256 devices in a mesh: tok: 64 (over z, x, core), grp: 4 (over y).
Axes of the slice: x: 4, y: 4, z: 8, core: 2. Of those that a mesh axis runs over, the one named last changes fastest.
Arguments:
- inputs: float32 [4, 8192, 1536], P('grp', 'tok'), may hold values from -6 to 6
- queries: bfloat16 [4, 8192, 1536], P('grp', 'tok'), may hold values from -100 to 100
- keys: bfloat16 [4, 8192, 256], P('grp', 'tok'), may hold values from -6 to 6
- values: bfloat16 [4, 8192, 256], P('grp', 'tok'), may hold values from -6 to 6
- prefix_keys: bfloat16 [2048, 256], P(('tok', 'grp')), may hold values from -7 to 7
- prefix_values: bfloat16 [2048, 256], P(('tok', 'grp')), may hold values from -6 to 6
- lengths: int32 [4, 16], replicated, may hold values from 1 to 4224, 8192 in all within a row
- out_weight: bfloat16 [1536, 1536], replicated, may hold values from -0.5 to 0.5
- norm_gain: float32 [1536], replicated, may hold values from 0.25 to 1.75
- router_weight: bfloat16 [1536, 32], replicated, may hold values from -0.15625 to 0.15625
- routes: int32 [4, 8192, 4], P('grp', 'tok'), may hold values from 0 to 31, all different within a row; in each aligned block of 128 rows (0 to 127, 128 to 255, ..., all dimensions but the last counted through in order) at most 24 rows name the same one
- expert_gate: bfloat16 [64, 1536, 384], P('tok'), may hold values from -0.15625 to 0.15625
- expert_up: bfloat16 [64, 1536, 384], P('tok'), may hold values from -0.15625 to 0.15625
- expert_down: bfloat16 [64, 384, 1536], P('tok'), may hold values from -0.21875 to 0.21875
Outputs:
- layer_out: float32 [4, 8192, 1536], P('grp', 'tok')
The draws below stay inside these ranges and needn't reach their ends.
Inputs may be any that keep to these rules, and one draw needn't show every extreme that they name: Row g holds the suffix lengths of the 16 requests of group g, in order; they sum to 8192, and the longest is exactly 4224. `routes`: each token names 4 different experts; of one device's 128 tokens no more than 24 name one expert, and in every draw some expert is named by exactly 24 of them.
All inputs are finite; a program needn't handle non-finite values.
Results may differ from the reference program's by a relative error of at most 0.0055.
Values may be sent and summed in bfloat16 or wider, within the bound.
A program may use at most 192 MiB of HBM per device.

```python
import math
import jax
import jax.numpy as jnp
import numpy as np
from jax import lax

D = 1536
HEADS = 12
KVH = 2
HD = 128
FF = 768
EXPERTS = 32
TOP = 4
TOK_DEV = 128
PREFIX = 2048
REQS = 16
SUFFIX = 8192
REQ_MAX = 4224
HSPLIT = 2
CAP = 24
KVW = 256
QW = 1536
N_TOK = 64
N_GRP = 4


def prefix_table(key):
    base = jnp.clip(jax.random.normal(jax.random.fold_in(key, 11), (PREFIX, KVW), jnp.float32), -4.0, 4.0) * 1.5
    return base


def draw_prefix_keys(key, part):
    return prefix_table(key).astype(jnp.bfloat16)


def draw_queries(key, part):
    drawn = jnp.clip(jax.random.normal(jax.random.fold_in(key, 23), (N_GRP, SUFFIX, QW), jnp.float32), -4.0, 4.0) * 1.5
    return drawn.astype(jnp.bfloat16)


def steps_of(key, dims, shards, low, top_value):
    factor_of, own = 1.0, jax.random.fold_in(key, 6)
    for dim, blocks in shards:
        heights = jnp.exp(jax.random.uniform(jax.random.fold_in(own, dim), (blocks,), jnp.float32, low / len(shards), top_value / len(shards)))
        factor_of = factor_of * jnp.repeat(heights, dims[dim] // blocks).reshape([-1 if axis == dim else 1 for axis in range(len(dims))])
    return factor_of


def length_profile(number_of, total, limit, slope):
    portions = [(1 << 20) // math.isqrt(rank ** slope) + 1 for rank in range(2, number_of + 1)]
    rest, holding = total - limit - (number_of - 1), [1] * (number_of - 1)
    while rest > 0:
        candidates = [i for i in range(number_of - 1) if holding[i] < limit]
        whole, left = sum([portions[i] for i in candidates]), rest
        for i in candidates:
            more = min(limit - holding[i], max(1, left * portions[i] // whole), rest)
            holding[i] = holding[i] + more
            rest = rest - more
    return np.array([limit] + holding)


def uneven(key, count, total, bound, lean):
    if count == 2:
        one = jax.random.randint(key, (), max(1, total - bound), min(bound, total - 1) + 1)
        return jnp.stack([one, total - one])
    sizes = jnp.asarray(length_profile(count, total, bound, lean), jnp.int32)
    twos = (count - 1) // 2
    source_of, taker = sizes[1:1 + 2 * twos:2], sizes[2:2 + 2 * twos:2]
    room = jnp.minimum(source_of - 1, bound - taker)
    moved = jax.random.randint(jax.random.fold_in(key, 1), (twos,), 0, 1 << 20) % (room + 1)
    sizes = sizes.at[1:1 + 2 * twos:2].set(source_of - moved).at[2:2 + 2 * twos:2].set(taker + moved)
    return sizes[jax.random.permutation(jax.random.fold_in(key, 2), count)]


def routed_block(stream_key, own, number, rows, amount, top, most, skew):
    sequence = jax.random.permutation(stream_key, amount)
    crowded, ordinary = portions_of(amount, rows * top, most, skew, True), portions_of(amount, rows * top, most, skew, False)
    places = jnp.arange(amount)

    def named(sizes, rotation):
        used = int((sizes > 0).sum())
        fixed = max(1, used // 4)
        moved = fixed + (places - fixed + rotation * (used - fixed)) % max(1, amount - fixed)
        return jnp.zeros((amount,), jnp.int32).at[sequence[jnp.where(places < fixed, places, moved)]].set(jnp.asarray(sizes, jnp.int32))

    sizes = jnp.where(number % 4 == 0, named(crowded, number // 4), named(ordinary, number - number // 4 - 1))
    mixed = jax.random.permutation(jax.random.fold_in(own, 3), amount)
    source_of, receiver = mixed[0:amount // 2 * 2:2], mixed[1:amount // 2 * 2:2]
    slack = jnp.minimum(sizes[source_of] - 1, most - sizes[receiver]) // 2
    slack = jnp.where((source_of == sequence[0]) | (receiver == sequence[0]) | (sizes[receiver] == 0), 0, jnp.maximum(slack, 0))
    moved = jax.random.randint(jax.random.fold_in(own, 4), (amount // 2,), 0, 1 << 20) % (slack + 1)
    sizes = sizes.at[source_of].add(-moved).at[receiver].add(moved)
    items = jnp.searchsorted(jnp.cumsum(sizes), jnp.arange(rows * top), side="right").astype(jnp.int32)
    listing = items.reshape(top, rows).T
    listing = listing[jax.random.permutation(jax.random.fold_in(own, 1), rows)]
    rotation = jax.random.randint(jax.random.fold_in(own, 2), (rows, 1), 0, top)
    return jnp.take_along_axis(listing, (jnp.arange(top)[None, :] + rotation) % top, axis=1)


def portions_of(number_of, total, most, lean, full):
    portions = [(1 << 20) // math.isqrt(rank ** lean) + 1 for rank in range(1, number_of + 1)]
    largest = most if full else min(most, max(-(-total // number_of), total * portions[0] // sum(portions)))
    least = 1 if total - largest >= number_of - 1 else 0
    given, spare = [largest] + [least] * (number_of - 1), total - largest - least * (number_of - 1)
    while spare > 0:
        candidates = [i for i in range(1, number_of) if given[i] < largest] or [i for i in range(1, number_of) if given[i] < most]
        pool, remaining = sum([portions[i] for i in candidates]), spare
        for i in candidates:
            addition = min(most - given[i], max(1, remaining * portions[i] // pool), spare)
            given[i] = given[i] + addition
            spare = spare - addition
    return np.array(given)


def normal_values(key, dims, width, limit, split=(), held_as=jnp.bfloat16):
    array = width * jax.random.normal(key, dims, jnp.float32)
    if split:
        array = array * steps_of(key, dims, split, -0.22, 0.18)
    return jnp.clip(array, -limit, limit).astype(held_as)


def setup_inputs(seed: int = 0) -> dict:
    key_of = jax.random.split(jax.random.key(seed), 15)
    inputs = normal_values(key_of[0], (N_GRP, SUFFIX, D), 1.0, 6.0, ((0, 4), (1, 64)), jnp.float32)
    queries = draw_queries(jax.random.fold_in(key_of[14], 71), 0)
    keys = normal_values(key_of[2], (N_GRP, SUFFIX, KVW), 1.5, 6.0, ((0, 4), (1, 64)))
    values = normal_values(key_of[3], (N_GRP, SUFFIX, KVW), 1.0, 6.0, ((0, 4), (1, 64)))
    prefix_keys = draw_prefix_keys(jax.random.fold_in(key_of[14], 71), 0)
    prefix_values = normal_values(key_of[5], (PREFIX, KVW), 1.0, 6.0, ((0, 256),))
    lengths = jax.vmap(lambda own: uneven(own, REQS, SUFFIX, REQ_MAX, 2))(jax.random.split(key_of[6], N_GRP)).reshape((N_GRP, REQS)).astype(jnp.int32)
    out_weight = normal_values(key_of[7], (QW, D), HD ** -0.5, 0.5)
    norm_gain = jnp.clip(1.0 + 0.15 * jax.random.normal(key_of[8], (D,), jnp.float32), 0.25, 1.75)
    router_weight = normal_values(key_of[9], (D, EXPERTS), D ** -0.5, 0.15625)
    routes_keys = jax.random.split(jax.random.fold_in(key_of[10], 1), N_GRP * SUFFIX // TOK_DEV)
    routes_turns = jax.random.permutation(jax.random.fold_in(key_of[10], 3), N_GRP * SUFFIX // TOK_DEV)
    routes = jax.vmap(lambda own, number: routed_block(jax.random.fold_in(key_of[10], 2), own, number, TOK_DEV, EXPERTS, TOP, CAP, 2))(routes_keys, routes_turns).reshape((N_GRP, SUFFIX, TOP))
    expert_gate = normal_values(key_of[11], (EXPERTS * HSPLIT, D, FF // HSPLIT), D ** -0.5, 0.15625, ((0, 64),))
    expert_up = normal_values(key_of[12], (EXPERTS * HSPLIT, D, FF // HSPLIT), D ** -0.5, 0.15625, ((0, 64),))
    expert_down = normal_values(key_of[13], (EXPERTS * HSPLIT, FF // HSPLIT, D), FF ** -0.5, 0.21875, ((0, 64),))
    return {"inputs": inputs, "queries": queries, "keys": keys, "values": values, "prefix_keys": prefix_keys, "prefix_values": prefix_values, "lengths": lengths, "out_weight": out_weight, "norm_gain": norm_gain, "router_weight": router_weight, "routes": routes, "expert_gate": expert_gate, "expert_up": expert_up, "expert_down": expert_down}


NEGATIVE = -1e+30

def request_starts(row_lengths, positions):
    request_ends = jnp.cumsum(row_lengths).astype(jnp.int32)
    passed = request_ends[None, :] <= positions[:, None]
    return lax.optimization_barrier(jnp.max(jnp.where(passed, request_ends[None, :], 0), axis=1)).astype(jnp.int32)

def reference(inputs, queries, keys, values, prefix_keys, prefix_values, lengths, out_weight, norm_gain, router_weight, routes, expert_gate, expert_up, expert_down):
    query_block = min(512, SUFFIX)
    window = min(SUFFIX, REQ_MAX + query_block)
    blocks = SUFFIX // query_block
    repeat = HEADS // KVH
    score_scale = 1.0 / math.sqrt(HD)
    high = lax.Precision.HIGHEST
    cached_keys = prefix_keys.astype(jnp.float32).reshape(PREFIX, KVH, HD)
    cached_values = prefix_values.astype(jnp.float32).reshape(PREFIX, KVH, HD)

    def attend(flat_index):
        group_index = (flat_index // blocks).astype(jnp.int32)
        first_query = (flat_index % blocks * query_block).astype(jnp.int32)
        group_queries = lax.dynamic_index_in_dim(queries, group_index, 0, keepdims=False)
        group_keys = lax.dynamic_index_in_dim(keys, group_index, 0, keepdims=False)
        group_values = lax.dynamic_index_in_dim(values, group_index, 0, keepdims=False)
        query_rows = lax.dynamic_slice_in_dim(group_queries, first_query, query_block, 0)
        query_rows = query_rows.astype(jnp.float32).reshape(query_block, KVH, repeat, HD)
        key_start = jnp.clip(first_query - REQ_MAX, 0, SUFFIX - window).astype(jnp.int32)
        window_keys = lax.dynamic_slice_in_dim(group_keys, key_start, window, 0).astype(jnp.float32).reshape(window, KVH, HD)
        window_values = lax.dynamic_slice_in_dim(group_values, key_start, window, 0).astype(jnp.float32).reshape(window, KVH, HD)
        query_positions = first_query + jnp.arange(query_block, dtype=jnp.int32)
        key_positions = key_start + jnp.arange(window, dtype=jnp.int32)
        row_lengths = lax.dynamic_index_in_dim(lengths, group_index, 0, keepdims=False)
        starts = request_starts(row_lengths, query_positions)
        valid = (key_positions[None, :] >= starts[:, None]) & (key_positions[None, :] <= query_positions[:, None])
        prefix_scores = jnp.einsum('tgrd,kgd->grtk', query_rows, cached_keys, precision=high) * score_scale
        suffix_scores = jnp.einsum('tgrd,kgd->grtk', query_rows, window_keys, precision=high) * score_scale
        masked = jnp.where(valid[None, None], suffix_scores, NEGATIVE)
        row_max = jnp.maximum(lax.optimization_barrier(jnp.max(prefix_scores, axis=-1)), lax.optimization_barrier(jnp.max(masked, axis=-1)))
        prefix_probs = jnp.exp(prefix_scores - row_max[..., None])
        suffix_probs = jnp.where(valid[None, None], jnp.exp(masked - row_max[..., None]), 0.0)
        row_total = lax.optimization_barrier(jnp.sum(prefix_probs, axis=-1)) + lax.optimization_barrier(jnp.sum(suffix_probs, axis=-1))
        prefix_round = lax.optimization_barrier(prefix_probs.astype(jnp.bfloat16)).astype(jnp.float32)
        suffix_round = lax.optimization_barrier(suffix_probs.astype(jnp.bfloat16)).astype(jnp.float32)
        numerator = jnp.einsum('grtk,kgd->grtd', prefix_round, cached_values, precision=high)
        numerator = numerator + jnp.einsum('grtk,kgd->grtd', suffix_round, window_values, precision=high)
        result = (numerator / row_total[..., None]).astype(jnp.bfloat16)
        return result.transpose(2, 0, 1, 3).reshape(query_block, QW)
    attended = lax.map(attend, jnp.arange(N_GRP * blocks, dtype=jnp.int32)).reshape(N_GRP * SUFFIX, QW)
    residual = inputs.reshape(N_GRP * SUFFIX, D) + jnp.dot(attended, out_weight, preferred_element_type=jnp.float32)
    normed = (residual * lax.rsqrt(lax.optimization_barrier(jnp.mean(residual * residual, axis=-1, keepdims=True)) + 1e-06) * norm_gain).astype(jnp.bfloat16)
    logits = jnp.dot(normed, router_weight, preferred_element_type=jnp.float32)
    route_table = routes.reshape(N_GRP * SUFFIX, TOP).astype(jnp.int32)
    sigmoids = jax.nn.sigmoid(jnp.take_along_axis(logits, route_table, axis=1))
    gate_weights = sigmoids / lax.optimization_barrier(jnp.sum(sigmoids, axis=1, keepdims=True))
    flat_routes = route_table.reshape(-1)
    sorted_pairs = jnp.argsort(flat_routes, stable=True).astype(jnp.int32)
    counts = lax.optimization_barrier(jnp.sum((flat_routes[:, None] == jnp.arange(EXPERTS, dtype=jnp.int32)[None, :]).astype(jnp.int32), axis=0))
    offsets = (jnp.cumsum(counts) - counts).astype(jnp.int32)
    most_rows = CAP * N_GRP * N_TOK
    padded = jnp.concatenate([sorted_pairs, jnp.zeros((most_rows,), jnp.int32)])
    gate_flat = gate_weights.reshape(-1)

    def expert_step(moe_total, expert):
        pair_index = lax.dynamic_slice_in_dim(padded, offsets[expert], most_rows, 0)
        live_rows = jnp.arange(most_rows, dtype=jnp.int32) < counts[expert]
        token_index = (pair_index // TOP).astype(jnp.int32)
        slot_rows = normed[token_index]
        result = jnp.zeros((most_rows, D), jnp.float32)
        for half_index in range(HSPLIT):
            slice_index = (expert * HSPLIT + half_index).astype(jnp.int32)
            gate_matrix = lax.dynamic_index_in_dim(expert_gate, slice_index, 0, keepdims=False)
            up_matrix = lax.dynamic_index_in_dim(expert_up, slice_index, 0, keepdims=False)
            down_matrix = lax.dynamic_index_in_dim(expert_down, slice_index, 0, keepdims=False)
            gated = jax.nn.relu(jnp.dot(slot_rows, gate_matrix, preferred_element_type=jnp.float32))
            hidden = (gated * jnp.dot(slot_rows, up_matrix, preferred_element_type=jnp.float32)).astype(jnp.bfloat16)
            part_out = jnp.dot(hidden, down_matrix, preferred_element_type=jnp.float32).astype(jnp.bfloat16)
            result = result + lax.optimization_barrier(part_out).astype(jnp.float32)
        result = lax.optimization_barrier(result.astype(jnp.bfloat16)).astype(jnp.float32)
        weight = jnp.where(live_rows, gate_flat[pair_index], 0.0)
        moe_total = moe_total.at[token_index].add(result * weight[:, None])
        return (moe_total, None)
    moe_total, _ = lax.scan(expert_step, jnp.zeros((N_GRP * SUFFIX, D), jnp.float32), jnp.arange(EXPERTS, dtype=jnp.int32))
    return (residual + moe_total).reshape(N_GRP, SUFFIX, D)
```

```python
import functools
import math

import jax
import jax.numpy as jnp
from jax import lax
from jax.experimental import pallas as pl
from jax.experimental.pallas import tpu as pltpu
from jax.sharding import Mesh, PartitionSpec as P

HEADS = 12
KVH = 2
HD = 128
REPEAT = HEADS // KVH
EXPERTS = 32
TOP = 4
CAP = 24
SLOTS = EXPERTS * CAP
ROWS = 128
KVW = KVH * HD
REACH = 34
CHUNK = 512
CHUNK_BLOCKS = CHUNK // ROWS
NEGATIVE = -1e30
SCALE = math.log2(math.e) / math.sqrt(HD)
F32 = jnp.float32
BF16 = jnp.bfloat16


def contract(left, right, left_dim, right_dim):
    return lax.dot_general(
        left, right, (((left_dim,), (right_dim,)), ((), ())), preferred_element_type=F32
    )


def attend_kernel(
    device_ref,
    inputs_ref,
    queries_ref,
    prefix_ref,
    suffix_ref,
    starts_ref,
    weight_hbm,
    gain_ref,
    router_ref,
    routes_ref,
    residual_ref,
    slots_ref,
    high_ref,
    low_ref,
    weight_ref,
    turned_ref,
    top_ref,
    total_ref,
    result_ref,
    weight_sem,
):
    weight_copy = pltpu.make_async_copy(weight_hbm, weight_ref, weight_sem)
    weight_copy.start()
    device = device_ref[0]
    width = REPEAT * ROWS
    for head in range(HEADS):
        group, place = head // REPEAT, head % REPEAT
        turned_ref[group, :, place * ROWS : (place + 1) * ROWS] = (
            queries_ref[:, head * HD : (head + 1) * HD].astype(F32).T.astype(BF16)
        )
    top_ref[...] = jnp.full_like(top_ref, NEGATIVE)
    total_ref[...] = jnp.zeros_like(total_ref)
    result_ref[...] = jnp.zeros_like(result_ref)

    def absorb(source, row, bias):
        for group in range(KVH):
            key_rows = source[pl.ds(row, CHUNK), group * HD : (group + 1) * HD]
            value_rows = source[pl.ds(row, CHUNK), KVW + group * HD : KVW + (group + 1) * HD]
            scores = contract(key_rows, turned_ref[group], 1, 0) * SCALE
            if bias is not None:
                scores = scores + jnp.concatenate([bias] * REPEAT, axis=1)
            old = top_ref[group]
            new = jnp.maximum(old, jnp.max(scores, axis=0, keepdims=True))
            factor = jnp.exp2(old - new)
            weights = jnp.exp2(scores - new)
            top_ref[group] = new
            total_ref[group] = total_ref[group] * factor + jnp.sum(weights, axis=0, keepdims=True)
            result_ref[group] = result_ref[group] * factor + contract(
                value_rows, weights.astype(BF16), 0, 0
            )

    def prefix_step(step, carry):
        absorb(prefix_ref, pl.multiple_of(step * CHUNK, CHUNK), None)
        return carry

    lax.fori_loop(0, prefix_ref.shape[0] // CHUNK, prefix_step, 0)

    positions = device * ROWS + lax.broadcasted_iota(jnp.int32, (1, ROWS), 1)
    starts = starts_ref[...]
    reached = jnp.minimum(device + 1, REACH)
    chunks = (reached + CHUNK_BLOCKS - 1) // CHUNK_BLOCKS
    first = jnp.maximum(device + 1 - chunks * CHUNK_BLOCKS, 0) * ROWS

    def suffix_step(step, carry):
        row = pl.multiple_of(first + step * CHUNK, ROWS)
        key_positions = row + lax.broadcasted_iota(jnp.int32, (CHUNK, ROWS), 0)
        valid = (key_positions >= starts) & (key_positions <= positions)
        absorb(suffix_ref, row, jnp.where(valid, 0.0, NEGATIVE))
        return carry

    lax.fori_loop(0, chunks, suffix_step, 0)

    weight_copy.wait()
    residual_ref[...] = inputs_ref[...]
    for group in range(KVH):
        attended = (result_ref[group] / total_ref[group]).T.astype(BF16)
        for place in range(REPEAT):
            head = group * REPEAT + place
            residual_ref[...] += jnp.dot(
                attended[place * ROWS : (place + 1) * ROWS],
                weight_ref[head * HD : (head + 1) * HD, :],
                preferred_element_type=F32,
            )
    residual = residual_ref[...]
    normed = (
        residual
        * lax.rsqrt(jnp.mean(residual * residual, axis=-1, keepdims=True) + 1e-06)
        * gain_ref[...]
    ).astype(BF16)

    expert_ids = lax.broadcasted_iota(jnp.int32, (EXPERTS, ROWS), 0)
    named = jnp.zeros((EXPERTS, ROWS), F32)
    for route in range(TOP):
        named = named + jnp.where(expert_ids == routes_ref[route : route + 1, :], 1.0, 0.0)
    earlier = (
        lax.broadcasted_iota(jnp.int32, (ROWS, ROWS), 0)
        < lax.broadcasted_iota(jnp.int32, (ROWS, ROWS), 1)
    )
    rank = jnp.dot(
        named.astype(BF16), jnp.where(earlier, 1.0, 0.0).astype(BF16), preferred_element_type=F32
    )
    rank = jnp.where(named > 0.5, rank, -1.0).astype(BF16)
    spread_row = lax.broadcasted_iota(jnp.int32, (SLOTS, EXPERTS), 0)
    spread_low = lax.broadcasted_iota(jnp.int32, (SLOTS, EXPERTS), 1) * CAP
    spread = jnp.where((spread_row >= spread_low) & (spread_row < spread_low + CAP), 1.0, 0.0).astype(
        BF16
    )
    slot_rank = jnp.dot(spread, rank, preferred_element_type=F32)
    slot_row = lax.broadcasted_iota(jnp.int32, (SLOTS, ROWS), 0)
    chosen = slot_rank == (slot_row % CAP).astype(F32)
    slots_ref[...] = jnp.dot(
        jnp.where(chosen, 1.0, 0.0).astype(BF16), normed, preferred_element_type=F32
    ).astype(BF16)

    logits = contract(router_ref[...], normed, 1, 1)
    sigmoids = named * jax.nn.sigmoid(logits)
    gates = sigmoids / jnp.sum(sigmoids, axis=0, keepdims=True)
    high = gates.astype(BF16)
    low = (gates - high.astype(F32)).astype(BF16)
    for part, part_ref in ((high, high_ref), (low, low_ref)):
        wide = jnp.dot(spread, part, preferred_element_type=F32)
        part_ref[...] = jnp.where(chosen, wide, 0.0).astype(BF16)


def attend(device, inputs, queries, prefix, suffix, starts, out_weight, gain, router, routes):
    rows, width = inputs.shape
    whole = pl.BlockSpec(memory_space=pltpu.VMEM)
    return pl.pallas_call(
        attend_kernel,
        out_shape=(
            jax.ShapeDtypeStruct((rows, width), F32),
            jax.ShapeDtypeStruct((SLOTS, width), BF16),
            jax.ShapeDtypeStruct((SLOTS, rows), BF16),
            jax.ShapeDtypeStruct((SLOTS, rows), BF16),
        ),
        in_specs=[
            pl.BlockSpec(memory_space=pltpu.SMEM),
            whole,
            whole,
            whole,
            whole,
            whole,
            pl.BlockSpec(memory_space=pl.ANY),
            whole,
            whole,
            whole,
        ],
        out_specs=(whole, whole, whole, whole),
        scratch_shapes=[
            pltpu.VMEM(out_weight.shape, BF16),
            pltpu.VMEM((KVH, HD, REPEAT * ROWS), BF16),
            pltpu.VMEM((KVH, 1, REPEAT * ROWS), F32),
            pltpu.VMEM((KVH, 1, REPEAT * ROWS), F32),
            pltpu.VMEM((KVH, HD, REPEAT * ROWS), F32),
            pltpu.SemaphoreType.DMA,
        ],
        compiler_params=pltpu.CompilerParams(vmem_limit_bytes=56 << 20),
        name="attend",
    )(device, inputs, queries, prefix, suffix, starts, out_weight, gain, router, routes)


def expert_kernel(rows_ref, gate_ref, up_ref, down_ref, out_ref, total_ref):
    step = pl.program_id(0)
    rows = rows_ref[...]
    gated = jax.nn.relu(jnp.dot(rows, gate_ref[0], preferred_element_type=F32))
    hidden = (gated * jnp.dot(rows, up_ref[0], preferred_element_type=F32)).astype(BF16)
    part = jnp.dot(hidden, down_ref[0], preferred_element_type=F32)

    @pl.when(step == 0)
    def _():
        total_ref[...] = part

    @pl.when(step > 0)
    def _():
        out_ref[...] = (total_ref[...] + part).astype(BF16)


def experts(rows, gate, up, down):
    count, width = rows.shape
    parts, _, hidden = gate.shape
    return pl.pallas_call(
        expert_kernel,
        grid=(parts,),
        out_shape=jax.ShapeDtypeStruct((count, width), BF16),
        in_specs=[
            pl.BlockSpec((count, width), lambda i: (0, 0)),
            pl.BlockSpec((1, width, hidden), lambda i: (i, 0, 0)),
            pl.BlockSpec((1, width, hidden), lambda i: (i, 0, 0)),
            pl.BlockSpec((1, hidden, width), lambda i: (i, 0, 0)),
        ],
        out_specs=pl.BlockSpec((count, width), lambda i: (0, 0)),
        scratch_shapes=[pltpu.VMEM((count, width), F32)],
        compiler_params=pltpu.CompilerParams(vmem_limit_bytes=48 << 20),
        name="experts",
    )(rows, gate, up, down)


def combine_kernel(residual_ref, high_ref, low_ref, results_ref, out_ref):
    results = results_ref[...]
    out_ref[...] = (
        residual_ref[...]
        + contract(high_ref[...], results, 0, 0)
        + contract(low_ref[...], results, 0, 0)
    )


def combine(residual, high, low, results):
    return pl.pallas_call(
        combine_kernel,
        out_shape=jax.ShapeDtypeStruct(residual.shape, F32),
        in_specs=[pl.BlockSpec(memory_space=pltpu.VMEM)] * 4,
        out_specs=pl.BlockSpec(memory_space=pltpu.VMEM),
        compiler_params=pltpu.CompilerParams(vmem_limit_bytes=32 << 20),
        name="combine",
    )(residual, high, low, results)


CHIPS = ("z", "x")
TOK = ("z", "x", "core")


def local(
    inputs,
    queries,
    keys,
    values,
    prefix_keys,
    prefix_values,
    lengths,
    out_weight,
    norm_gain,
    router_weight,
    routes,
    expert_gate,
    expert_up,
    expert_down,
):
    swap = [(0, 1), (1, 0)]
    gate = jnp.concatenate([expert_gate, lax.ppermute(expert_gate, "core", swap)])
    up = jnp.concatenate([expert_up, lax.ppermute(expert_up, "core", swap)])
    down = jnp.concatenate([expert_down, lax.ppermute(expert_down, "core", swap)])
    prefix = lax.all_gather(
        jnp.concatenate([prefix_keys, prefix_values], axis=1), TOK + ("grp",), axis=0, tiled=True
    )
    suffix = lax.all_gather(
        jnp.concatenate([keys[0], values[0]], axis=1), TOK, axis=0, tiled=True
    )
    device = lax.axis_index(TOK)
    positions = device * ROWS + jnp.arange(ROWS, dtype=jnp.int32)
    row_lengths = lax.dynamic_index_in_dim(lengths, lax.axis_index("grp"), 0, keepdims=False)
    request_ends = jnp.cumsum(row_lengths)
    starts = jnp.max(
        jnp.where(request_ends[None, :] <= positions[:, None], request_ends[None, :], 0), axis=1
    )
    residual, slots, high, low = attend(
        device.reshape(1).astype(jnp.int32),
        inputs[0],
        queries[0],
        prefix,
        suffix,
        starts.astype(jnp.int32)[None, :],
        out_weight,
        norm_gain[None, :],
        router_weight.T,
        routes[0].T,
    )
    width = inputs.shape[2]
    arrived = lax.all_to_all(
        slots.reshape(EXPERTS, CAP, width), CHIPS, split_axis=0, concat_axis=0, tiled=True
    )
    computed = experts(arrived.reshape(SLOTS, width), gate, up, down)
    returned = lax.all_to_all(
        computed.reshape(EXPERTS, CAP, width), CHIPS, split_axis=0, concat_axis=0, tiled=True
    )
    return combine(residual, high, low, returned.reshape(SLOTS, width))[None]


def solution(mesh):
    fine = Mesh(mesh.devices.reshape(8, 4, 2, 4), ("z", "x", "core", "grp"))
    placed = (
        P("grp", TOK, None),
        P("grp", TOK, None),
        P("grp", TOK, None),
        P("grp", TOK, None),
        P(TOK + ("grp",), None),
        P(TOK + ("grp",), None),
        P(),
        P(),
        P(),
        P(),
        P("grp", TOK, None),
        P(TOK, None, None),
        P(TOK, None, None),
        P(TOK, None, None),
    )
    return jax.shard_map(
        local, mesh=fine, in_specs=placed, out_specs=P("grp", TOK, None), check_vma=False
    )
```

```python
import functools
import math

import jax
import jax.numpy as jnp
from jax import lax
from jax.experimental import pallas as pl
from jax.experimental.pallas import tpu as pltpu
from jax.sharding import Mesh, PartitionSpec as P

HEADS = 12
KVH = 2
HD = 128
REPEAT = HEADS // KVH
EXPERTS = 32
TOP = 4
CAP = 24
SLOTS = EXPERTS * CAP
ROWS = 128
KVW = KVH * HD
CHUNK = 512
NEGATIVE = -1e30
SCALE = math.log2(math.e) / math.sqrt(HD)
F32 = jnp.float32
BF16 = jnp.bfloat16


def contract(left, right, left_dim, right_dim):
    return lax.dot_general(
        left, right, (((left_dim,), (right_dim,)), ((), ())), preferred_element_type=F32
    )


Z, X, Y, CORES = 8, 4, 4, 2
PLANES = 5
SUB = 64
SUBS = CHUNK // SUB
PREFIX_CHUNKS = 2
SUFFIX_CHUNKS = CORES * PLANES
TICKS = CORES * (PLANES + PREFIX_CHUNKS)
EARLY = 6
MESH = pl.DeviceIdType.MESH


def attend_kernel(
    lengths_ref,
    inputs_hbm,
    queries_hbm,
    keys_hbm,
    values_hbm,
    prefix_keys_hbm,
    prefix_values_hbm,
    weight_hbm,
    gain_ref,
    router_ref,
    routes_ref,
    residual_ref,
    slots_ref,
    high_ref,
    low_ref,
    weight_ref,
    queries_ref,
    turned_ref,
    top_ref,
    total_ref,
    result_ref,
    held,
    corner,
    local_sem,
    z_send,
    z_recv,
    x_send,
    x_recv,
    half_send,
    half_recv,
    core_send,
    core_recv,
    pz_send,
    pz_recv,
    px_send,
    px_recv,
    py_send,
    py_recv,
    pc_send,
    pc_recv,
    corner_send,
    corner_recv,
):
    z, x = lax.axis_index("z"), lax.axis_index("x")
    core, y = lax.axis_index("core"), lax.axis_index("grp")
    device = (z * X + x) * CORES + core
    other = 1 - core
    right, left, across = lax.rem(x + 1, X), lax.rem(x + X - 1, X), lax.rem(x + 2, X)

    def chunk_of(which, plane):
        return which * PLANES + plane

    def block(plane, place):
        return held.at[chunk_of(core, plane), pl.ds(2 * place, 2)]

    def half(plane, place, kind):
        return held.at[chunk_of(core, plane), pl.ds(2 * place, 2), kind]

    def prefix_chunk(which, row):
        return SUFFIX_CHUNKS + which * PREFIX_CHUNKS + row // 2

    def prefix_sub(row, place):
        return lax.rem(row, 2) * X + place

    mine = prefix_chunk(core, y)
    loads = [
        pltpu.make_async_copy(keys_hbm, half(0, x, 0), local_sem.at[0]),
        pltpu.make_async_copy(values_hbm, half(0, x, 1), local_sem.at[1]),
        pltpu.make_async_copy(
            prefix_keys_hbm,
            held.at[mine, prefix_sub(y, x), 0, pl.ds(pl.multiple_of(z * 8, 8), 8)],
            local_sem.at[2],
        ),
        pltpu.make_async_copy(
            prefix_values_hbm,
            held.at[mine, prefix_sub(y, x), 1, pl.ds(pl.multiple_of(z * 8, 8), 8)],
            local_sem.at[3],
        ),
        pltpu.make_async_copy(queries_hbm, queries_ref, local_sem.at[4]),
        pltpu.make_async_copy(inputs_hbm, residual_ref, local_sem.at[5]),
        pltpu.make_async_copy(weight_hbm, weight_ref, local_sem.at[6]),
    ]
    for load in loads:
        load.start()

    barrier = pltpu.get_barrier_semaphore()
    for step in range(1, Z):
        pl.semaphore_signal(
            barrier, inc=1, device_id={"z": lax.rem(z + step, Z)}, device_id_type=MESH
        )
    for step in range(1, X):
        pl.semaphore_signal(
            barrier, inc=1, device_id={"x": lax.rem(x + step, X)}, device_id_type=MESH
        )
    for step in range(1, Y):
        pl.semaphore_signal(
            barrier, inc=1, device_id={"grp": lax.rem(y + step, Y)}, device_id_type=MESH
        )
    pl.semaphore_signal(barrier, inc=1, device_id={"core": other}, device_id_type=MESH)
    gives = (x == X - 1) & (core == 1)
    takes = (x == 0) & (core == 0)
    corner_to = {"z": lax.rem(z + PLANES, Z), "x": 0, "core": 0}
    corner_from = {"z": lax.rem(z + Z - PLANES, Z), "x": X - 1, "core": 1}

    @pl.when(gives)
    def _():
        pl.semaphore_signal(barrier, inc=1, device_id=corner_to, device_id_type=MESH)

    @pl.when(takes)
    def _():
        pl.semaphore_signal(barrier, inc=1, device_id=corner_from, device_id_type=MESH)

    greeted = (Z - 1) + (X - 1) + (Y - 1) + 1
    pl.semaphore_wait(barrier, greeted + jnp.where(gives | takes, 1, 0))

    def remote(source, target, send, recv, where):
        return pltpu.make_async_remote_copy(
            src_ref=source,
            dst_ref=target,
            send_sem=send,
            recv_sem=recv,
            device_id=where,
            device_id_type=MESH,
        )

    def z_copy(plane, place):
        return remote(
            block(plane - 1, place),
            block(plane, place),
            z_send.at[plane],
            z_recv.at[plane],
            {"z": lax.rem(z + 1, Z)},
        )

    def x_copy(plane, way, place):
        return remote(
            block(plane, place),
            block(plane, place),
            x_send.at[plane, way],
            x_recv.at[plane, way],
            {"x": right if way == 0 else left},
        )

    def half_copy(plane, way, place):
        return remote(
            half(plane, place, way),
            half(plane, place, way),
            half_send.at[plane, way],
            half_recv.at[plane, way],
            {"x": right if way == 0 else left},
        )

    def core_copy(plane, which):
        return remote(
            held.at[chunk_of(which, plane)],
            held.at[chunk_of(which, plane)],
            core_send.at[plane],
            core_recv.at[plane],
            {"core": other},
        )

    def pz_copy(step, place):
        region = held.at[mine, prefix_sub(y, x), :, pl.ds(pl.multiple_of(place * 8, 8), 8)]
        return remote(
            region, region, pz_send.at[step], pz_recv.at[step], {"z": lax.rem(z + step, Z)}
        )

    def px_copy(step, place):
        region = held.at[mine, prefix_sub(y, place)]
        return remote(
            region, region, px_send.at[step], px_recv.at[step], {"x": lax.rem(x + step, X)}
        )

    def py_copy(step, place):
        region = held.at[
            prefix_chunk(core, place), pl.ds(pl.multiple_of(lax.rem(place, 2) * X, X), X)
        ]
        return remote(
            region, region, py_send.at[step], py_recv.at[step], {"grp": lax.rem(y + step, Y)}
        )

    def pc_copy(which):
        region = held.at[pl.ds(SUFFIX_CHUNKS + which * PREFIX_CHUNKS, PREFIX_CHUNKS)]
        return remote(region, region, pc_send, pc_recv, {"core": other})

    corner_copy = remote(block(0, x), corner, corner_send, corner_recv, corner_to)

    def z_start(plane):
        z_copy(plane, x).start()

    def z_done(plane):
        z_copy(plane, x).wait_recv()

    def x_start(plane):
        for way in range(2):
            x_copy(plane, way, x).start()

    def x_turn(plane):
        for way, place in ((0, left), (1, right)):
            x_copy(plane, way, place).wait_recv()
            half_copy(plane, way, place).start()

    def core_start(plane):
        for way in range(2):
            half_copy(plane, way, across).wait_recv()
        core_copy(plane, core).start()

    def core_done(plane):
        core_copy(plane, other).wait_recv()

    def px_start():
        for step in range(1, Z):
            pz_copy(step, lax.rem(z + Z - step, Z)).wait_recv()
        for step in range(1, X):
            px_copy(step, x).start()

    def py_start():
        for step in range(1, X):
            px_copy(step, lax.rem(x + X - step, X)).wait_recv()
        for step in range(1, Y):
            py_copy(step, y).start()

    def pc_start():
        for step in range(1, Y):
            py_copy(step, lax.rem(y + Y - step, Y)).wait_recv()
        pc_copy(core).start()

    for load in loads[:2]:
        load.wait()
    z_start(1)
    x_start(0)
    for load in loads[2:4]:
        load.wait()
    for step in range(1, Z):
        pz_copy(step, z).start()

    @pl.when(gives)
    def _():
        corner_copy.start()

    loads[4].wait()
    for head in range(HEADS):
        group, place = head // REPEAT, head % REPEAT
        turned_ref[group, :, place * ROWS : (place + 1) * ROWS] = (
            queries_ref[:, head * HD : (head + 1) * HD].astype(F32).T.astype(BF16)
        )
    top_ref[...] = jnp.full_like(top_ref, NEGATIVE)
    total_ref[...] = jnp.zeros_like(total_ref)
    result_ref[...] = jnp.zeros_like(result_ref)
    positions = device * ROWS + lax.broadcasted_iota(jnp.int32, (1, ROWS), 1)
    starts = jnp.zeros((1, ROWS), jnp.int32)
    end = 0
    for request in range(lengths_ref.shape[1]):
        end = end + lengths_ref[y, request]
        starts = jnp.where(end <= positions, end, starts)

    def absorb(keys_of, values_of, bias):
        for group in range(KVH):
            key_rows, value_rows = keys_of(group), values_of(group)
            scores = contract(key_rows, turned_ref[group], 1, 0) * SCALE
            scores = scores + jnp.concatenate([bias] * REPEAT, axis=1)
            old = top_ref[group]
            new = jnp.maximum(old, jnp.max(scores, axis=0, keepdims=True))
            factor = jnp.exp2(old - new)
            weights = jnp.exp2(scores - new)
            top_ref[group] = new
            total_ref[group] = total_ref[group] * factor + jnp.sum(weights, axis=0, keepdims=True)
            result_ref[group] = result_ref[group] * factor + contract(
                value_rows, weights.astype(BF16), 0, 0
            )

    z_done(1)
    z_start(2)
    x_start(1)
    x_turn(0)
    px_start()
    core_start(0)

    actions = {
        1: [(core_done, 0), (z_done, 2), (z_start, 3), (x_start, 2), (x_turn, 1), (py_start,)],
        2: [(core_start, 1), (z_done, 3), (z_start, 4), (x_start, 3)],
        3: [(core_done, 1), (x_turn, 2)],
        4: [(core_start, 2), (z_done, 4), (x_start, 4)],
        5: [(core_done, 2), (x_turn, 3), (pc_start,)],
        6: [(core_start, 3)],
        7: [(x_turn, 4)],
        8: [(lambda: pc_copy(other).wait_recv(),), (core_start, 4)],
        10: [(core_done, 3)],
        13: [(core_done, 4)],
    }

    def act(tick):
        for action, *rest in actions[tick]:
            action(*rest)

    def tick_step(tick, carry):
        for known in actions:
            pl.when(tick == known)(functools.partial(act, known))
        late = tick >= EARLY + CORES * PREFIX_CHUNKS
        cached = (tick >= EARLY) & jnp.logical_not(late)
        counted = jnp.where(late, tick - CORES * PREFIX_CHUNKS, tick)
        plane = counted // CORES
        which = lax.rem(core + lax.rem(counted, CORES), CORES)
        cached_step = tick - EARLY
        cached_which = lax.rem(core + cached_step // PREFIX_CHUNKS, CORES)
        chunk = jnp.where(
            cached,
            SUFFIX_CHUNKS + cached_which * PREFIX_CHUNKS + lax.rem(cached_step + 2, PREFIX_CHUNKS),
            chunk_of(which, plane),
        )
        row = lax.broadcasted_iota(jnp.int32, (CHUNK, ROWS), 0)
        base = jnp.where(cached, 0, ((z - plane) * X * CORES + which) * ROWS)
        key_positions = base + row + (row - lax.rem(row, ROWS))
        low = jnp.where(cached, jnp.zeros_like(starts), starts)
        high = jnp.where(cached, jnp.full_like(positions, 1 << 20), positions)
        valid = (key_positions >= low) & (key_positions <= high)

        def part(kind):
            return lambda group: held[chunk, :, kind, :, group * HD : (group + 1) * HD].reshape(
                CHUNK, HD
            )

        absorb(part(0), part(1), jnp.where(valid, 0.0, NEGATIVE))
        return carry

    lax.fori_loop(0, TICKS, tick_step, 0)

    @pl.when(takes)
    def _():
        corner_copy.wait_recv()
        row = lax.broadcasted_iota(jnp.int32, (ROWS, ROWS), 0)
        key_positions = ((z - PLANES) * X * CORES + X * CORES - 1) * ROWS + row
        valid = (key_positions >= starts) & (key_positions <= positions)

        def part(kind):
            return lambda group: corner[:, kind, :, group * HD : (group + 1) * HD].reshape(ROWS, HD)

        absorb(part(0), part(1), jnp.where(valid, 0.0, NEGATIVE))

    for load in loads[5:]:
        load.wait()
    for group in range(KVH):
        attended = (result_ref[group] / total_ref[group]).T.astype(BF16)
        for place in range(REPEAT):
            head = group * REPEAT + place
            residual_ref[...] += jnp.dot(
                attended[place * ROWS : (place + 1) * ROWS],
                weight_ref[head * HD : (head + 1) * HD, :],
                preferred_element_type=F32,
            )
    residual = residual_ref[...]
    normed = (
        residual
        * lax.rsqrt(jnp.mean(residual * residual, axis=-1, keepdims=True) + 1e-06)
        * gain_ref[...]
    ).astype(BF16)

    expert_ids = lax.broadcasted_iota(jnp.int32, (EXPERTS, ROWS), 0)
    named = jnp.zeros((EXPERTS, ROWS), F32)
    for route in range(TOP):
        named = named + jnp.where(expert_ids == routes_ref[route : route + 1, :], 1.0, 0.0)
    earlier = (
        lax.broadcasted_iota(jnp.int32, (ROWS, ROWS), 0)
        < lax.broadcasted_iota(jnp.int32, (ROWS, ROWS), 1)
    )
    rank = jnp.dot(
        named.astype(BF16), jnp.where(earlier, 1.0, 0.0).astype(BF16), preferred_element_type=F32
    )
    rank = jnp.where(named > 0.5, rank, -1.0).astype(BF16)
    spread_row = lax.broadcasted_iota(jnp.int32, (SLOTS, EXPERTS), 0)
    spread_low = lax.broadcasted_iota(jnp.int32, (SLOTS, EXPERTS), 1) * CAP
    spread = jnp.where((spread_row >= spread_low) & (spread_row < spread_low + CAP), 1.0, 0.0).astype(
        BF16
    )
    slot_rank = jnp.dot(spread, rank, preferred_element_type=F32)
    slot_row = lax.broadcasted_iota(jnp.int32, (SLOTS, ROWS), 0)
    chosen = slot_rank == (slot_row % CAP).astype(F32)
    slots_ref[...] = jnp.dot(
        jnp.where(chosen, 1.0, 0.0).astype(BF16), normed, preferred_element_type=F32
    ).astype(BF16)

    logits = contract(router_ref[...], normed, 1, 1)
    sigmoids = named * jax.nn.sigmoid(logits)
    gates = sigmoids / jnp.sum(sigmoids, axis=0, keepdims=True)
    high = gates.astype(BF16)
    low = (gates - high.astype(F32)).astype(BF16)
    for part, part_ref in ((high, high_ref), (low, low_ref)):
        wide = jnp.dot(spread, part, preferred_element_type=F32)
        part_ref[...] = jnp.where(chosen, wide, 0.0).astype(BF16)

    for plane in range(1, PLANES):
        z_copy(plane, x).wait_send()
    for plane in range(PLANES):
        for way, place in ((0, left), (1, right)):
            x_copy(plane, way, x).wait_send()
            half_copy(plane, way, place).wait_send()
        core_copy(plane, core).wait_send()
    for step in range(1, Z):
        pz_copy(step, z).wait_send()
    for step in range(1, X):
        px_copy(step, x).wait_send()
    for step in range(1, Y):
        py_copy(step, y).wait_send()
    pc_copy(core).wait_send()

    @pl.when(gives)
    def _():
        corner_copy.wait_send()


def attend(
    lengths, inputs, queries, keys, values, prefix_keys, prefix_values, out_weight, gain, router, routes
):
    rows, width = inputs.shape
    whole = pl.BlockSpec(memory_space=pltpu.VMEM)
    apart = pl.BlockSpec(memory_space=pl.ANY)
    wires = pltpu.SemaphoreType.DMA
    pairs = [(PLANES,), (PLANES, 2), (PLANES, 2), (PLANES,), (Z,), (X,), (Y,), (), ()]
    return pl.pallas_call(
        attend_kernel,
        out_shape=(
            jax.ShapeDtypeStruct((rows, width), F32),
            jax.ShapeDtypeStruct((SLOTS, width), BF16),
            jax.ShapeDtypeStruct((SLOTS, rows), BF16),
            jax.ShapeDtypeStruct((SLOTS, rows), BF16),
        ),
        in_specs=[pl.BlockSpec(memory_space=pltpu.SMEM)] + [apart] * 7 + [whole] * 3,
        out_specs=(whole, whole, whole, whole),
        scratch_shapes=[
            pltpu.VMEM(out_weight.shape, BF16),
            pltpu.VMEM(queries.shape, BF16),
            pltpu.VMEM((KVH, HD, REPEAT * ROWS), BF16),
            pltpu.VMEM((KVH, 1, REPEAT * ROWS), F32),
            pltpu.VMEM((KVH, 1, REPEAT * ROWS), F32),
            pltpu.VMEM((KVH, HD, REPEAT * ROWS), F32),
            pltpu.VMEM((TICKS, SUBS, 2, SUB, KVW), BF16),
            pltpu.VMEM((ROWS // SUB, 2, SUB, KVW), BF16),
            wires((7,)),
        ]
        + [wires(shape) if shape else wires for shape in pairs for _ in range(2)],
        compiler_params=pltpu.CompilerParams(
            vmem_limit_bytes=56 << 20, collective_id=0, has_side_effects=True
        ),
        name="attend",
    )(
        lengths,
        inputs,
        queries,
        keys.reshape(ROWS // SUB, SUB, KVW),
        values.reshape(ROWS // SUB, SUB, KVW),
        prefix_keys,
        prefix_values,
        out_weight,
        gain,
        router,
        routes,
    )


def expert_kernel(rows_ref, *refs):
    out_ref = refs[-1]
    rows = rows_ref[...]
    total = None
    for gate_ref, up_ref, down_ref in (refs[0:3], refs[3:6]):
        gated = jax.nn.relu(jnp.dot(rows, gate_ref[0], preferred_element_type=F32))
        hidden = (gated * jnp.dot(rows, up_ref[0], preferred_element_type=F32)).astype(BF16)
        part = jnp.dot(hidden, down_ref[0], preferred_element_type=F32)
        total = part if total is None else total + part
    out_ref[...] = total.astype(BF16)


def experts(rows, *weights):
    count, width = rows.shape
    tile = 256
    held = [pl.BlockSpec(weight.shape, lambda i: (0, 0, 0)) for weight in weights]
    return pl.pallas_call(
        expert_kernel,
        grid=(count // tile,),
        out_shape=jax.ShapeDtypeStruct((count, width), BF16),
        in_specs=[pl.BlockSpec((tile, width), lambda i: (i, 0))] + held,
        out_specs=pl.BlockSpec((tile, width), lambda i: (i, 0)),
        compiler_params=pltpu.CompilerParams(vmem_limit_bytes=48 << 20),
        name="experts",
    )(rows, *weights)


def combine_kernel(residual_ref, high_ref, low_ref, results_ref, out_ref):
    results = results_ref[...]
    out_ref[...] = (
        residual_ref[...]
        + contract(high_ref[...], results, 0, 0)
        + contract(low_ref[...], results, 0, 0)
    )


def combine(residual, high, low, results):
    return pl.pallas_call(
        combine_kernel,
        out_shape=jax.ShapeDtypeStruct(residual.shape, F32),
        in_specs=[pl.BlockSpec(memory_space=pltpu.VMEM)] * 4,
        out_specs=pl.BlockSpec(memory_space=pltpu.VMEM),
        compiler_params=pltpu.CompilerParams(vmem_limit_bytes=32 << 20),
        name="combine",
    )(residual, high, low, results)


CHIPS = ("z", "x")
TOK = ("z", "x", "core")


def local(
    inputs,
    queries,
    keys,
    values,
    prefix_keys,
    prefix_values,
    lengths,
    out_weight,
    norm_gain,
    router_weight,
    routes,
    expert_gate,
    expert_up,
    expert_down,
):
    own = (expert_gate, expert_up, expert_down)
    partner = tuple(lax.ppermute(weight, "core", [(0, 1), (1, 0)]) for weight in own)
    residual, slots, high, low = attend(
        lengths,
        inputs[0],
        queries[0],
        keys[0],
        values[0],
        prefix_keys,
        prefix_values,
        out_weight,
        norm_gain[None, :],
        router_weight.T,
        routes[0].T,
    )
    width = inputs.shape[2]
    arrived = lax.all_to_all(
        slots.reshape(EXPERTS, CAP, width), CHIPS, split_axis=0, concat_axis=0, tiled=True
    )
    computed = experts(arrived.reshape(SLOTS, width), *own, *partner)
    returned = lax.all_to_all(
        computed.reshape(EXPERTS, CAP, width), CHIPS, split_axis=0, concat_axis=0, tiled=True
    )
    return combine(residual, high, low, returned.reshape(SLOTS, width))[None]


def solution(mesh):
    fine = Mesh(mesh.devices.reshape(8, 4, 2, 4), ("z", "x", "core", "grp"))
    placed = (
        P("grp", TOK, None),
        P("grp", TOK, None),
        P("grp", TOK, None),
        P("grp", TOK, None),
        P(TOK + ("grp",), None),
        P(TOK + ("grp",), None),
        P(),
        P(),
        P(),
        P(),
        P("grp", TOK, None),
        P(TOK, None, None),
        P(TOK, None, None),
        P(TOK, None, None),
    )
    return jax.shard_map(
        local, mesh=fine, in_specs=placed, out_specs=P("grp", TOK, None), check_vma=False
    )
```
